32 devices in a mesh: gy: 4 (over y, x), gx: 8 (over z, core).
Axes of the slice: x: 2, y: 2, z: 4, core: 2. Of those that a mesh axis runs over, the one named last changes fastest.
Arguments:
- window_starts: int32 [4, 8, 2, 4], P('gy', 'gx'), may hold values from -64 to 192, as said below
- slot_counts: int32 [4, 8], P('gy', 'gx'), may hold values from 2 to 4, as said below
- intensities: float32 [4, 8, 4, 128, 128], P('gy', 'gx'), may hold values from 0 to 1
- probe_field: float32 [2, 128, 128], replicated, may hold values from -3 to 3
- kernel_phase: float32 [128, 128], replicated, may hold values from -3.140625 to 3.140625
- object_field: float32 [2, 2, 1024, 2048], P(None, None, 'gy', 'gx'), may hold values from -4.2 to 4.2
Outputs:
- estimate: float32 [2, 2, 1024, 2048], P(None, None, 'gy', 'gx')
- gradient: float32 [2, 2, 1024, 2048], P(None, None, 'gy', 'gx')
The draws below stay inside these ranges and needn't reach their ends.
Inputs may be any that keep to these rules, and one draw needn't show every extreme that they name: `slot_counts`: slots 0 to the count minus one of a tile are live, the rest unused. `window_starts`: A slot's window covers 128 x 128 cells from its start, in cells relative to the tile's first cell. In every tile, slot 0's window starts above the tile's first row and reaches past its last column; slot 1's window reaches past its last row and starts left of its first column.
All inputs are finite; a program needn't handle non-finite values.
Results may differ from the reference program's by a relative error of at most 0.0003.
Values sent between devices are 32-bit elements; how exact they have to be, the bound alone decides.
A program may use at most 64 MiB of HBM per device.

```python
import math
import jax
import jax.numpy as jnp
from jax import lax

W = 128
TILE = 256
RIM = 64
GROUPS = 4
CAP = 4
ITERS = 2
TILES_Y = 4
TILES_X = 8
NY = 1024
NX = 2048


def draw_slot_counts(key, part):
    key_light, key_heavy, key_band = jax.random.split(key, 3)
    light_load = jax.random.randint(key_light, (TILES_Y, TILES_X), 2, max(3, CAP // 2 + 1))
    heavy_load = jax.random.randint(key_heavy, (TILES_Y, TILES_X), max(2, CAP // 2 + 1), CAP + 1)
    band_start = jax.random.randint(key_band, (TILES_Y, 1), 0, TILES_X)
    columns = jnp.arange(TILES_X, dtype=jnp.int32)[None, :]
    tile_rows = jnp.arange(TILES_Y, dtype=jnp.int32)[:, None]
    band_width = max(1, TILES_X // 8)
    in_band = (columns - band_start) % TILES_X < band_width
    loads = jnp.where(in_band, heavy_load, light_load)
    first_tile = (tile_rows == 0) & (columns == band_start)
    loads = jnp.where(first_tile, CAP, loads)
    quiet_tile = (tile_rows == 0) & (columns == (band_start + band_width) % TILES_X)
    loads = jnp.where(quiet_tile, 2, loads)
    return loads.astype(jnp.int32)


def draw_window_starts(key, part):
    key_all, key_low, key_high = jax.random.split(jax.random.fold_in(key, 11), 3)
    offsets = jax.random.randint(key_all, (TILES_Y, TILES_X, 2, CAP), -RIM, TILE - RIM + 1)
    low_part = jax.random.randint(key_low, (TILES_Y, TILES_X, 2), -RIM, 0)
    high_part = jax.random.randint(key_high, (TILES_Y, TILES_X, 2), TILE - W + 1, TILE - RIM + 1)
    offsets = offsets.at[:, :, 0, 0].set(low_part[:, :, 0])
    offsets = offsets.at[:, :, 1, 0].set(high_part[:, :, 0])
    offsets = offsets.at[:, :, 0, 1].set(high_part[:, :, 1])
    offsets = offsets.at[:, :, 1, 1].set(low_part[:, :, 1])
    offsets = offsets.at[0, 0, 0, 0].set(-RIM)
    offsets = offsets.at[0, 0, 1, 0].set(TILE - RIM)
    return offsets.astype(jnp.int32)


def shard_levels(key, dims, shards, low, high):
    loudness, own = 1.0, jax.random.fold_in(key, 6)
    for position, shards_of in shards:
        heights = jnp.exp(jax.random.uniform(jax.random.fold_in(own, position), (shards_of,), jnp.float32, low / len(shards), high / len(shards)))
        loudness = loudness * jnp.repeat(heights, dims[position] // shards_of).reshape([-1 if axis == position else 1 for axis in range(len(dims))])
    return loudness


def centred(rng, dims, width, limit, shards=(), held_as=jnp.bfloat16):
    entries = jax.random.normal(rng, dims, jnp.float32) * width
    if len(shards) > 0:
        entries = shard_levels(rng, dims, shards, -0.22, 0.18) * entries
    return jnp.clip(entries, min=-limit, max=limit).astype(held_as)


def setup_inputs(seed: int = 0) -> dict:
    seeds = jax.random.split(jax.random.key(seed), 7)
    return {
        "window_starts": draw_window_starts(jax.random.fold_in(seeds[6], 71), 0),
        "slot_counts": draw_slot_counts(jax.random.fold_in(seeds[6], 71), 0),
        "intensities": jnp.clip(1.0 * jax.random.uniform(seeds[2], (TILES_Y, TILES_X, CAP, W, W), jnp.float32) ** shard_levels(seeds[2], (TILES_Y, TILES_X, CAP, W, W), ((0, 4), (1, 8)), -0.2, 0.2), 0.0, 1.0),
        "probe_field": centred(seeds[3], (2, W, W), 0.5, 3.0, (), jnp.float32),
        "kernel_phase": jnp.clip(jax.random.uniform(seeds[4], (W, W), jnp.float32, -3.140625, 3.140625), -3.140625, 3.140625),
        "object_field": centred(seeds[5], (2, 2, NY, NX), 0.7, 4.2, ((2, 4), (3, 8)), jnp.float32),
    }


highest = lax.Precision.HIGHEST
step_size = 0.5

def fourier_tables(window):
    cell_index = jnp.arange(window, dtype=jnp.int32)
    product = cell_index[:, None] * cell_index[None, :] % window
    phase_grid = 2.0 * math.pi / window * product.astype(jnp.float32)
    scale_factor = 1.0 / math.sqrt(window)
    return (jnp.cos(phase_grid) * scale_factor, -jnp.sin(phase_grid) * scale_factor)

def transform(field_r, field_i, table_r, table_i):
    left_r = jnp.einsum('jk,nkl->njl', table_r, field_r, precision=highest) - jnp.einsum('jk,nkl->njl', table_i, field_i, precision=highest)
    left_i = jnp.einsum('jk,nkl->njl', table_r, field_i, precision=highest) + jnp.einsum('jk,nkl->njl', table_i, field_r, precision=highest)
    out_r = jnp.einsum('njk,kl->njl', left_r, table_r, precision=highest) - jnp.einsum('njk,kl->njl', left_i, table_i, precision=highest)
    out_i = jnp.einsum('njk,kl->njl', left_r, table_i, precision=highest) + jnp.einsum('njk,kl->njl', left_i, table_r, precision=highest)
    return (out_r, out_i)

def slot_gradients(windows, intensity, probe_field, kernel_r, kernel_i, table_r, table_i):
    first_r, first_i = (windows[:, 0], windows[:, 1])
    second_r, second_i = (windows[:, 2], windows[:, 3])
    probe_r, probe_i = (probe_field[0], probe_field[1])
    wave_r = probe_r * first_r - probe_i * first_i
    wave_i = probe_r * first_i + probe_i * first_r
    spec_r, spec_i = transform(wave_r, wave_i, table_r, table_i)
    prop_r = kernel_r * spec_r - kernel_i * spec_i
    prop_i = kernel_r * spec_i + kernel_i * spec_r
    phi_r, phi_i = transform(prop_r, prop_i, table_r, -table_i)
    chi_r = phi_r * second_r - phi_i * second_i
    chi_i = phi_r * second_i + phi_i * second_r
    far_r, far_i = transform(chi_r, chi_i, table_r, table_i)
    excess = far_r * far_r + far_i * far_i - intensity
    back_r, back_i = transform(excess * far_r, excess * far_i, table_r, -table_i)
    grad_two_r = phi_r * back_r + phi_i * back_i
    grad_two_i = phi_r * back_i - phi_i * back_r
    gphi_r = second_r * back_r + second_i * back_i
    gphi_i = second_r * back_i - second_i * back_r
    fwd_r, fwd_i = transform(gphi_r, gphi_i, table_r, table_i)
    conj_r = kernel_r * fwd_r + kernel_i * fwd_i
    conj_i = kernel_r * fwd_i - kernel_i * fwd_r
    gpsi_r, gpsi_i = transform(conj_r, conj_i, table_r, -table_i)
    grad_one_r = probe_r * gpsi_r + probe_i * gpsi_i
    grad_one_i = probe_r * gpsi_i - probe_i * gpsi_r
    return jnp.stack([grad_one_r, grad_one_i, grad_two_r, grad_two_i], axis=1)

def tile_gradient(extended, offsets, live_count, intensity, probe_field, kernel_r, kernel_i, table_r, table_i):
    window = probe_field.shape[-1]
    rim_cells = window // 2
    slot_total = offsets.shape[1]
    per_group = slot_total // GROUPS
    starts = (offsets + rim_cells).astype(jnp.int32)
    anchor = jnp.zeros((), jnp.int32)

    def take_window(row_start, col_start):
        return lax.dynamic_slice(extended, (anchor, row_start, col_start), (4, window, window))
    windows = jax.vmap(take_window)(starts[0], starts[1])
    pieces = []
    for group_index in range(GROUPS):
        first_slot = group_index * per_group
        group_windows = windows[first_slot:first_slot + per_group]
        group_intensity = intensity[first_slot:first_slot + per_group]
        pieces.append(lax.cond(live_count > first_slot, lambda: slot_gradients(group_windows, group_intensity, probe_field, kernel_r, kernel_i, table_r, table_i), lambda: jnp.zeros_like(group_windows)))
    live_mask = (jnp.arange(slot_total) < live_count).astype(jnp.float32)
    slot_grads = jnp.concatenate(pieces, axis=0) * live_mask[:, None, None, None]

    def add_one(slot_index, accumulated):
        row_start = starts[0, slot_index]
        col_start = starts[1, slot_index]
        current = lax.dynamic_slice(accumulated, (anchor, row_start, col_start), (4, window, window))
        return lax.dynamic_update_slice(accumulated, current + slot_grads[slot_index], (anchor, row_start, col_start))
    return lax.fori_loop(0, slot_total, add_one, jnp.zeros(extended.shape, jnp.float32))

def fold_wrap(accumulated):
    core = accumulated[:, RIM:RIM + NY, :]
    core = core.at[:, 0:RIM, :].add(accumulated[:, RIM + NY:, :])
    core = core.at[:, NY - RIM:, :].add(accumulated[:, :RIM, :])
    inner = core[:, :, RIM:RIM + NX]
    inner = inner.at[:, :, 0:RIM].add(core[:, :, RIM + NX:])
    inner = inner.at[:, :, NX - RIM:].add(core[:, :, :RIM])
    return inner

def reference(window_starts, slot_counts, intensities, probe_field, kernel_phase, object_field):
    table_r, table_i = fourier_tables(W)
    kernel_r = jnp.cos(kernel_phase)
    kernel_i = jnp.sin(kernel_phase)
    planes = object_field.reshape(4, NY, NX)
    tile_rows = jnp.repeat(jnp.arange(TILES_Y, dtype=jnp.int32), TILES_X)
    tile_cols = jnp.tile(jnp.arange(TILES_X, dtype=jnp.int32), TILES_Y)
    inputs = (tile_rows, tile_cols, window_starts.reshape(TILES_Y * TILES_X, 2, CAP), slot_counts.reshape(TILES_Y * TILES_X), intensities.reshape(TILES_Y * TILES_X, CAP, W, W))
    anchor = jnp.zeros((), jnp.int32)
    gradient = jnp.zeros_like(planes)
    for iteration in range(ITERS):
        padded = jnp.pad(planes, ((0, 0), (RIM, RIM), (RIM, RIM)), mode='wrap')

        def visit_tile(accumulated, tile_inputs):
            tile_row, tile_col, offsets, live_count, intensity = tile_inputs
            corner = (anchor, (tile_row * TILE).astype(jnp.int32), (tile_col * TILE).astype(jnp.int32))
            extended = lax.dynamic_slice(padded, corner, (4, TILE + 2 * RIM, TILE + 2 * RIM))
            grad_ext = tile_gradient(extended, offsets, live_count, intensity, probe_field, kernel_r, kernel_i, table_r, table_i)
            current = lax.dynamic_slice(accumulated, corner, grad_ext.shape)
            return (lax.dynamic_update_slice(accumulated, current + grad_ext, corner), None)
        accumulated, unused = lax.scan(visit_tile, jnp.zeros(padded.shape, jnp.float32), inputs)
        gradient = fold_wrap(accumulated)
        planes = planes - step_size * gradient
    return (planes.reshape(2, 2, NY, NX), gradient.reshape(2, 2, NY, NX))
```

```python
import functools
import math

import jax
import jax.numpy as jnp
import numpy as np
from jax import lax
from jax.experimental import pallas as pl
from jax.experimental.pallas import tpu as pltpu
from jax.sharding import PartitionSpec as P

ITERS = 2
LANES = 128
MESH = pl.DeviceIdType.MESH

step_size = 0.5
HALO, FOLD = 0, 1
BACK, AHEAD = 0, 1


def split(table):
    high = table.astype(jnp.bfloat16)
    low = (table - high.astype(np.float32)).astype(jnp.bfloat16)
    return high, low


def fourier_tables(window):
    cells = np.arange(window)
    phase = 2.0 * math.pi / window * (cells[:, None] * cells[None, :] % window)
    real = np.cos(phase) / math.sqrt(window)
    rights, lefts = [], []
    for sign in (-1.0, 1.0):
        imag = sign * np.sin(phase) / math.sqrt(window)
        right = np.block([[real, imag], [-imag, real]]).astype(np.float32)
        high, low = split(right)
        rights.append(np.concatenate([high, high, low], axis=0))
        high, low = split(np.ascontiguousarray(right.T))
        lefts.append(np.concatenate([high, low, high], axis=1))
    return np.stack(rights), np.stack(lefts)


def halves(x):
    high = x.astype(jnp.bfloat16)
    low = (x - high.astype(jnp.float32)).astype(jnp.bfloat16)
    return high, low


def transform(fields, right, left):
    size = fields[0][0].shape[0]
    count = len(fields)
    rows = jnp.concatenate([jnp.concatenate(f, axis=1) for f in fields], axis=0)
    high, low = halves(rows)
    rows = jnp.dot(
        jnp.concatenate([high, low, high], axis=1), right[...], preferred_element_type=jnp.float32
    )
    cols = jnp.concatenate(
        [
            jnp.concatenate(
                [
                    rows[n * size : (n + 1) * size, :size],
                    rows[n * size : (n + 1) * size, size:],
                ],
                axis=0,
            )
            for n in range(count)
        ],
        axis=1,
    )
    high, low = halves(cols)
    cols = jnp.dot(
        left[...], jnp.concatenate([high, high, low], axis=0), preferred_element_type=jnp.float32
    )
    return [
        (cols[:size, n * size : (n + 1) * size], cols[size:, n * size : (n + 1) * size])
        for n in range(count)
    ]


def times(a, b):
    return (a[0] * b[0] - a[1] * b[1], a[0] * b[1] + a[1] * b[0])


def conj_times(a, b):
    return (a[0] * b[0] + a[1] * b[1], a[0] * b[1] - a[1] * b[0])


def kernel(
    sizes,
    starts_ref,
    count_ref,
    inten_ref,
    probe_ref,
    prop_ref,
    right_ref,
    left_ref,
    obj_ref,
    est_ref,
    grad_ref,
    ext,
    acc,
    row_pick,
    row_place,
    col_pick,
    col_place,
    col_out,
    col_in,
    row_in,
    send_sem,
    recv_sem,
):
    rows_axis, cols_axis, window = sizes
    tile = obj_ref.shape[-1]
    rim = window // 2
    slots = inten_ref.shape[2]
    rows_all = tile + 2 * rim
    lane0 = LANES
    inner = slice(lane0, lane0 + tile)
    wide = tile + 2 * LANES
    my, mx = lax.axis_index("gy"), lax.axis_index("gx")
    up = {"gy": lax.rem(my + rows_axis - 1, rows_axis)}
    down = {"gy": lax.rem(my + 1, rows_axis)}
    west = {"gx": lax.rem(mx + cols_axis - 1, cols_axis)}
    east = {"gx": lax.rem(mx + 1, cols_axis)}

    barrier = pltpu.get_barrier_semaphore()
    for other in (up, down, west, east):
        pl.semaphore_signal(barrier, inc=1, device_id=other, device_id_type=MESH)
    pl.semaphore_wait(barrier, 4)

    def remote(src, dst, it, what, s, part, direction):
        k = ((((it * 2) + what) * 2 + s) * 3 + part) * 2 + direction
        dev = ((west, east), (west, east), (up, down))[part][direction]
        return pltpu.make_async_remote_copy(
            src_ref=src,
            dst_ref=dst,
            send_sem=send_sem.at[k],
            recv_sem=recv_sem.at[k],
            device_id=dev,
            device_id_type=MESH,
        )

    def col_copy(it, what, s, part, direction):
        span = pl.ds(0, tile) if part == 0 else pl.ds(tile, 2 * rim)
        at = (it, what, s, direction, span)
        return remote(col_out.at[at], col_in.at[at], it, what, s, part, direction)

    def halo_rows(it, s, direction):
        first = 0 if direction == BACK else tile - rim
        if it == 0:
            src = obj_ref.at[s, :, pl.ds(first, rim), :]
        else:
            src = ext.at[it, s, :, pl.ds(rim + first, rim), pl.ds(lane0, tile)]
        land = tile + rim if direction == BACK else 0
        dst = ext.at[it, s, :, pl.ds(land, rim), pl.ds(lane0, tile)]
        return remote(src, dst, it, HALO, s, 2, direction)

    def fold_rows(it, s, direction):
        first = 0 if direction == BACK else tile + rim
        src = acc.at[it, s, :, pl.ds(first, rim), pl.ds(lane0, tile)]
        return remote(src, row_in.at[it, s, direction], it, FOLD, s, 2, direction)

    def low_lanes(shape):
        return lax.broadcasted_iota(jnp.int32, shape, 1) < rim

    def turned(x):
        return pltpu.roll(x, rim, 1)

    def pack_low(re, im):
        return jnp.where(low_lanes(re.shape), re, turned(im))

    def pack_high(re, im):
        return jnp.where(low_lanes(re.shape), turned(re), im)

    sent = []

    def start(copy):
        copy.start()
        sent.append(copy)

    mid_pieces = ((0, rim, tile),)
    rim_pieces = ((tile, 0, rim), (tile + rim, tile + rim, rim))

    def halo_cols(it, s, part):
        for at, first, length in mid_pieces if part == 0 else rim_pieces:
            src = ext.at[it, s]
            rows = pl.ds(first, length)
            re, im = (src[c, rows, lane0 : lane0 + LANES] for c in range(2))
            col_out[it, HALO, s, BACK, pl.ds(at, length), :] = pack_low(re, im)
            re, im = (src[c, rows, lane0 + tile - LANES : lane0 + tile] for c in range(2))
            col_out[it, HALO, s, AHEAD, pl.ds(at, length), :] = pack_high(re, im)
        for direction in (BACK, AHEAD):
            start(col_copy(it, HALO, s, part, direction))

    def unpack_halo(it, s):
        for at, first, length in mid_pieces + rim_pieces:
            rows = pl.ds(first, length)
            got = col_in[it, HALO, s, AHEAD, pl.ds(at, length), :]
            ext[it, s, 0, rows, 0:LANES] = turned(got)
            ext[it, s, 1, rows, 0:LANES] = got
            got = col_in[it, HALO, s, BACK, pl.ds(at, length), :]
            ext[it, s, 0, rows, lane0 + tile : wide] = got
            ext[it, s, 1, rows, lane0 + tile : wide] = turned(got)

    def halo_start(it, s):
        for direction in (BACK, AHEAD):
            start(halo_rows(it, s, direction))
        halo_cols(it, s, 0)

    def halo_corners(it, s):
        for direction in (BACK, AHEAD):
            halo_rows(it, s, direction).wait_recv()
        halo_cols(it, s, 1)

    def halo_finish(it, s):
        for part in (0, 1):
            for direction in (BACK, AHEAD):
                col_copy(it, HALO, s, part, direction).wait_recv()
        unpack_halo(it, s)

    def ones(mask):
        return jnp.where(mask, 1.0, 0.0).astype(jnp.bfloat16)

    def build_picks():
        for j in range(slots):
            row = starts_ref[0, 0, 0, j] + rim
            col = starts_ref[0, 0, 1, j] + lane0
            span = slice(j * window, (j + 1) * window)
            for ref, at, first, shape, sign in (
                (row_pick, (span, slice(None)), row, (window, rows_all), 1),
                (row_place, (slice(None), span), row, (rows_all, window), -1),
                (col_pick, (slice(None), span), col, (wide, window), -1),
                (col_place, (span, slice(None)), col, (window, wide), 1),
            ):
                across = lax.broadcasted_iota(jnp.int32, shape, 1)
                along = lax.broadcasted_iota(jnp.int32, shape, 0)
                live = jnp.full(shape, count_ref[0, 0], jnp.int32) > j
                ref[at] = ones((sign * (across - along) == first) & live)

    def crop(it, s):
        both = jnp.concatenate([ext[it, s, c] for c in range(2)], axis=0)
        high, low = halves(both)
        cols = jnp.dot(
            jnp.concatenate([high, low], axis=1),
            jnp.concatenate([col_pick[...], col_pick[...]], axis=0),
            preferred_element_type=jnp.float32,
        )
        high, low = halves(cols)
        out = []
        for j in range(slots):
            span = slice(j * window, (j + 1) * window)
            pick = row_pick[span, :]
            field = [
                jnp.concatenate([part[:rows_all, span], part[rows_all:, span]], axis=1)
                for part in (high, low)
            ]
            got = jnp.dot(
                jnp.concatenate([pick, pick], axis=1),
                jnp.concatenate(field, axis=0),
                preferred_element_type=jnp.float32,
            )
            out.append((got[:, :window], got[:, window:]))
        return out

    def scatter(it, s, grads):
        parts = []
        for j in range(slots):
            span = slice(j * window, (j + 1) * window)
            put = row_place[:, span]
            high, low = halves(jnp.concatenate(grads[j], axis=1))
            got = jnp.dot(
                jnp.concatenate([put, put], axis=1),
                jnp.concatenate([high, low], axis=0),
                preferred_element_type=jnp.float32,
            )
            parts.append(jnp.concatenate([got[:, :window], got[:, window:]], axis=0))
        high, low = halves(jnp.concatenate(parts, axis=1))
        total = jnp.dot(
            jnp.concatenate([high, low], axis=1),
            jnp.concatenate([col_place[...], col_place[...]], axis=0),
            preferred_element_type=jnp.float32,
        )
        acc[it, s, 0] = total[:rows_all]
        acc[it, s, 1] = total[rows_all:]

    def fold_start(it, s):
        src = acc.at[it, s]
        for part, pieces in ((1, rim_pieces), (0, mid_pieces)):
            for at, first, length in pieces:
                rows = pl.ds(first, length)
                re, im = (src[c, rows, 0:LANES] for c in range(2))
                col_out[it, FOLD, s, BACK, pl.ds(at, length), :] = pack_high(re, im)
                re, im = (src[c, rows, lane0 + tile : wide] for c in range(2))
                col_out[it, FOLD, s, AHEAD, pl.ds(at, length), :] = pack_low(re, im)
            for direction in (BACK, AHEAD):
                start(col_copy(it, FOLD, s, part, direction))

    def add_cols(it, s, pieces):
        for at, first, length in pieces:
            rows = pl.ds(first, length)
            low = low_lanes((length, LANES))
            got = col_in[it, FOLD, s, AHEAD, pl.ds(at, length), :]
            lanes = slice(lane0, lane0 + LANES)
            acc[it, s, 0, rows, lanes] += jnp.where(low, got, 0.0)
            acc[it, s, 1, rows, lanes] += jnp.where(low, turned(got), 0.0)
            got = col_in[it, FOLD, s, BACK, pl.ds(at, length), :]
            lanes = slice(lane0 + tile - LANES, lane0 + tile)
            acc[it, s, 0, rows, lanes] += jnp.where(low, 0.0, turned(got))
            acc[it, s, 1, rows, lanes] += jnp.where(low, 0.0, got)

    def fold_corners(it, s):
        for direction in (BACK, AHEAD):
            col_copy(it, FOLD, s, 1, direction).wait_recv()
        add_cols(it, s, rim_pieces)
        for direction in (BACK, AHEAD):
            start(fold_rows(it, s, direction))

    def fold_finish(it, s):
        for direction in (BACK, AHEAD):
            col_copy(it, FOLD, s, 0, direction).wait_recv()
        add_cols(it, s, mid_pieces)
        for direction in (BACK, AHEAD):
            fold_rows(it, s, direction).wait_recv()
        last = it == ITERS - 1
        for c in range(2):
            for first in range(0, tile, rim):
                total = acc[it, s, c, pl.ds(rim + first, rim), inner]
                if first == 0:
                    total += row_in[it, s, AHEAD, c]
                if first == tile - rim:
                    total += row_in[it, s, BACK, c]
                new = ext[it, s, c, pl.ds(rim + first, rim), inner] - step_size * total
                if last:
                    grad_ref[s, c, pl.ds(first, rim), :] = total
                    est_ref[s, c, pl.ds(first, rim), :] = new
                else:
                    ext[it + 1, s, c, pl.ds(rim + first, rim), inner] = new

    for s in range(2):
        for direction in (BACK, AHEAD):
            start(halo_rows(0, s, direction))
    for s in range(2):
        for c in range(2):
            ext[0, s, c, rim : rim + tile, inner] = obj_ref[s, c]
        halo_cols(0, s, 0)
    build_picks()

    forward = (right_ref.at[0], left_ref.at[0])
    inverse = (right_ref.at[1], left_ref.at[1])

    for it in range(ITERS):
        halo_corners(it, 0)
        halo_finish(it, 0)
        probe = (probe_ref[0], probe_ref[1])
        prop = (prop_ref[0], prop_ref[1])
        waves = [times(probe, a) for a in crop(it, 0)]
        waves = [times(prop, f) for f in transform(waves, *forward)]
        halo_corners(it, 1)
        phi = transform(waves, *inverse)
        halo_finish(it, 1)
        second = crop(it, 1)
        far = transform([times(p, a) for p, a in zip(phi, second)], *forward)
        resid = []
        for j, (re, im) in enumerate(far):
            excess = re * re + im * im - inten_ref[0, 0, j]
            resid.append((excess * re, excess * im))
        back = transform(resid, *inverse)
        scatter(it, 1, [conj_times(p, b) for p, b in zip(phi, back)])
        fold_start(it, 1)
        waves = transform([conj_times(a, b) for a, b in zip(second, back)], *forward)
        fold_corners(it, 1)
        waves = transform([conj_times(prop, f) for f in waves], *inverse)
        scatter(it, 0, [conj_times(probe, g) for g in waves])
        fold_start(it, 0)
        fold_corners(it, 0)
        fold_finish(it, 1)
        if it + 1 < ITERS:
            halo_start(it + 1, 1)
        fold_finish(it, 0)
        if it + 1 < ITERS:
            halo_start(it + 1, 0)
    for copy in sent:
        copy.wait_send()


def local(sizes, window_starts, slot_counts, intensities, probe_field, kernel_phase, object_field):
    tile = object_field.shape[-1]
    window = sizes[2]
    rim = window // 2
    rows_all = tile + 2 * rim
    wide = tile + 2 * LANES
    slots = intensities.shape[2]
    right, left = fourier_tables(window)
    prop = jnp.stack([jnp.cos(kernel_phase), jnp.sin(kernel_phase)])
    vmem = pl.BlockSpec(memory_space=pltpu.VMEM)
    smem = pl.BlockSpec(memory_space=pltpu.SMEM)
    copies = ITERS * 2 * 2 * 3 * 2
    shape = jax.ShapeDtypeStruct(object_field.shape, jnp.float32)
    return pl.pallas_call(
        functools.partial(kernel, sizes),
        out_shape=(shape, shape),
        in_specs=[smem, smem] + [vmem] * 6,
        out_specs=(vmem, vmem),
        scratch_shapes=[
            pltpu.VMEM((ITERS, 2, 2, rows_all, wide), jnp.float32),
            pltpu.VMEM((ITERS, 2, 2, rows_all, wide), jnp.float32),
            pltpu.VMEM((slots * window, rows_all), jnp.bfloat16),
            pltpu.VMEM((rows_all, slots * window), jnp.bfloat16),
            pltpu.VMEM((wide, slots * window), jnp.bfloat16),
            pltpu.VMEM((slots * window, wide), jnp.bfloat16),
            pltpu.VMEM((ITERS, 2, 2, 2, rows_all, LANES), jnp.float32),
            pltpu.VMEM((ITERS, 2, 2, 2, rows_all, LANES), jnp.float32),
            pltpu.VMEM((ITERS, 2, 2, 2, rim, tile), jnp.float32),
            pltpu.SemaphoreType.DMA((copies,)),
            pltpu.SemaphoreType.DMA((copies,)),
        ],
        compiler_params=pltpu.CompilerParams(
            collective_id=0, has_side_effects=True, vmem_limit_bytes=56 * 1024 * 1024
        ),
    )(
        window_starts,
        slot_counts,
        intensities,
        probe_field,
        prop,
        jnp.asarray(right),
        jnp.asarray(left),
        object_field,
    )


def solution(mesh):
    in_specs = (
        P("gy", "gx", None, None),
        P("gy", "gx"),
        P("gy", "gx", None, None, None),
        P(),
        P(),
        P(None, None, "gy", "gx"),
    )
    out_specs = (P(None, None, "gy", "gx"), P(None, None, "gy", "gx"))

    def run(*args):
        sizes = (mesh.shape["gy"], mesh.shape["gx"], args[3].shape[-1])
        return jax.shard_map(
            functools.partial(local, sizes),
            mesh=mesh,
            in_specs=in_specs,
            out_specs=out_specs,
            check_vma=False,
        )(*args)

    return run
```

```python
import functools
import math

import jax
import jax.numpy as jnp
import numpy as np
from jax import lax
from jax.experimental import pallas as pl
from jax.experimental.pallas import tpu as pltpu
from jax.sharding import PartitionSpec as P

ITERS = 2
LANES = 128
MESH = pl.DeviceIdType.MESH

step_size = 0.5
HALO, FOLD = 0, 1
BACK, AHEAD = 0, 1
MID, TOP, BOTTOM, ROWS = 0, 1, 2, 3


def split(table):
    high = table.astype(jnp.bfloat16)
    low = (table - high.astype(np.float32)).astype(jnp.bfloat16)
    return high, low


def fourier_tables(window):
    cells = np.arange(window)
    phase = 2.0 * math.pi / window * (cells[:, None] * cells[None, :] % window)
    real = np.cos(phase) / math.sqrt(window)
    rights, lefts = [], []
    for sign in (-1.0, 1.0):
        imag = sign * np.sin(phase) / math.sqrt(window)
        right = np.block([[real, imag], [-imag, real]]).astype(np.float32)
        high, low = split(right)
        rights.append(np.concatenate([high, high, low], axis=0))
        high, low = split(np.ascontiguousarray(right.T))
        lefts.append(np.concatenate([high, low, high], axis=1))
    return np.stack(rights), np.stack(lefts)


def halves(x):
    high = x.astype(jnp.bfloat16)
    low = (x - high.astype(jnp.float32)).astype(jnp.bfloat16)
    return high, low


def transform(fields, right, left):
    size = fields[0][0].shape[0]
    count = len(fields)
    rows = jnp.concatenate([jnp.concatenate(f, axis=1) for f in fields], axis=0)
    high, low = halves(rows)
    rows = jnp.dot(
        jnp.concatenate([high, low, high], axis=1), right[...], preferred_element_type=jnp.float32
    )
    cols = jnp.concatenate(
        [
            jnp.concatenate(
                [
                    rows[n * size : (n + 1) * size, :size],
                    rows[n * size : (n + 1) * size, size:],
                ],
                axis=0,
            )
            for n in range(count)
        ],
        axis=1,
    )
    high, low = halves(cols)
    cols = jnp.dot(
        left[...], jnp.concatenate([high, high, low], axis=0), preferred_element_type=jnp.float32
    )
    return [
        (cols[:size, n * size : (n + 1) * size], cols[size:, n * size : (n + 1) * size])
        for n in range(count)
    ]


def times(a, b):
    return (a[0] * b[0] - a[1] * b[1], a[0] * b[1] + a[1] * b[0])


def conj_times(a, b):
    return (a[0] * b[0] + a[1] * b[1], a[0] * b[1] - a[1] * b[0])


def phasor(angle):
    x = 0.5 * angle
    y = x * x
    sine, cosine = 0.0, 0.0
    for k in range(7, -1, -1):
        sine = sine * y + (-1.0) ** k / math.factorial(2 * k + 1)
        cosine = cosine * y + (-1.0) ** k / math.factorial(2 * k)
    sine = sine * x
    return (1.0 - 2.0 * sine * sine, 2.0 * sine * cosine)


def kernel(
    sizes,
    starts_ref,
    count_ref,
    inten_ref,
    probe_ref,
    phase_ref,
    right_ref,
    left_ref,
    obj_ref,
    old_ref,
    change_ref,
    ext,
    acc,
    row_pick,
    row_place,
    col_pick,
    col_place,
    col_out,
    col_in,
    row_in,
    send_sem,
    recv_sem,
):
    rows_axis, cols_axis, window = sizes
    tile = obj_ref.shape[-1]
    rim = window // 2
    slots = inten_ref.shape[2]
    rows_all = tile + 2 * rim
    lane0 = LANES
    inner = slice(lane0, lane0 + tile)
    wide = tile + 2 * LANES
    my, mx = lax.axis_index("gy"), lax.axis_index("gx")
    up = {"gy": lax.rem(my + rows_axis - 1, rows_axis)}
    down = {"gy": lax.rem(my + 1, rows_axis)}
    west = {"gx": lax.rem(mx + cols_axis - 1, cols_axis)}
    east = {"gx": lax.rem(mx + 1, cols_axis)}

    barrier = pltpu.get_barrier_semaphore()
    for other in (up, down, west, east):
        pl.semaphore_signal(barrier, inc=1, device_id=other, device_id_type=MESH)
    pl.semaphore_wait(barrier, 4)

    def remote(src, dst, it, what, s, part, direction):
        k = ((((it * 2) + what) * 2 + s) * 4 + part) * 2 + direction
        dev = (up, down)[direction] if part == ROWS else (west, east)[direction]
        return pltpu.make_async_remote_copy(
            src_ref=src,
            dst_ref=dst,
            send_sem=send_sem.at[k],
            recv_sem=recv_sem.at[k],
            device_id=dev,
            device_id_type=MESH,
        )

    pieces = {
        MID: (0, rim, tile),
        TOP: (tile, 0, rim),
        BOTTOM: (tile + rim, tile + rim, rim),
    }
    own, rims = (MID,), (TOP, BOTTOM)

    def col_copy(it, what, s, part, direction):
        at = (it, what, s, direction, pl.ds(pieces[part][0], pieces[part][2]))
        return remote(col_out.at[at], col_in.at[at], it, what, s, part, direction)

    def halo_rows(it, s, direction):
        first = 0 if direction == BACK else tile - rim
        if it == 0:
            src = obj_ref.at[s, :, pl.ds(first, rim), :]
        else:
            src = ext.at[it, s, :, pl.ds(rim + first, rim), pl.ds(lane0, tile)]
        land = tile + rim if direction == BACK else 0
        dst = ext.at[it, s, :, pl.ds(land, rim), pl.ds(lane0, tile)]
        return remote(src, dst, it, HALO, s, ROWS, direction)

    def fold_rows(it, s, direction):
        first = 0 if direction == BACK else tile + rim
        src = acc.at[it, s, :, pl.ds(first, rim), pl.ds(lane0, tile)]
        return remote(src, row_in.at[it, s, direction], it, FOLD, s, ROWS, direction)

    def low_lanes(shape):
        return lax.broadcasted_iota(jnp.int32, shape, 1) < rim

    def turned(x):
        return pltpu.roll(x, rim, 1)

    def pack_low(re, im):
        return jnp.where(low_lanes(re.shape), re, turned(im))

    def pack_high(re, im):
        return jnp.where(low_lanes(re.shape), turned(re), im)

    sent = []

    def start(copy):
        copy.start()
        sent.append(copy)

    def halo_cols(it, s, part):
        at, first, length = pieces[part]
        src = ext.at[it, s]
        rows = pl.ds(first, length)
        re, im = (src[c, rows, lane0 : lane0 + LANES] for c in range(2))
        col_out[it, HALO, s, BACK, pl.ds(at, length), :] = pack_low(re, im)
        re, im = (src[c, rows, lane0 + tile - LANES : lane0 + tile] for c in range(2))
        col_out[it, HALO, s, AHEAD, pl.ds(at, length), :] = pack_high(re, im)
        for direction in (BACK, AHEAD):
            start(col_copy(it, HALO, s, part, direction))

    def halo_arrive(it, s, parts):
        for part in parts:
            at, first, length = pieces[part]
            for direction in (BACK, AHEAD):
                col_copy(it, HALO, s, part, direction).wait_recv()
            rows = pl.ds(first, length)
            got = col_in[it, HALO, s, AHEAD, pl.ds(at, length), :]
            ext[it, s, 0, rows, 0:LANES] = turned(got)
            ext[it, s, 1, rows, 0:LANES] = got
            got = col_in[it, HALO, s, BACK, pl.ds(at, length), :]
            ext[it, s, 0, rows, lane0 + tile : wide] = got
            ext[it, s, 1, rows, lane0 + tile : wide] = turned(got)

    def halo_start(it, s):
        for direction in (BACK, AHEAD):
            start(halo_rows(it, s, direction))
        halo_cols(it, s, MID)

    def halo_corners(it, s):
        for direction, part in ((BACK, BOTTOM), (AHEAD, TOP)):
            halo_rows(it, s, direction).wait_recv()
            halo_cols(it, s, part)

    def ones(mask):
        return jnp.where(mask, 1.0, 0.0).astype(jnp.bfloat16)

    def ext_row(k):
        return jnp.where(k < tile, k + rim, jnp.where(k < tile + rim, k - tile, k))

    def build_picks():
        for j in range(slots):
            row = starts_ref[0, 0, 0, j] + rim
            col = starts_ref[0, 0, 1, j] + lane0
            span = slice(j * window, (j + 1) * window)

            def build(shape, large, small, first, order):
                large = order(lax.broadcasted_iota(jnp.int32, shape, large))
                small = lax.broadcasted_iota(jnp.int32, shape, small)
                live = jnp.full(shape, count_ref[0, 0], jnp.int32) > j
                return ones((large - small == first) & live)

            row_pick[span, :] = build((window, rows_all), 1, 0, row, ext_row)
            row_place[:, span] = build((rows_all, window), 0, 1, row, ext_row)
            col_pick[:, span] = build((wide, window), 0, 1, col, lambda k: k)
            col_place[span, :] = build((window, wide), 1, 0, col, lambda k: k)

    def crop(it, s, parts):
        begin = pieces[parts[0]][0]
        height = sum(pieces[part][2] for part in parts)
        both = jnp.concatenate(
            [
                ext[it, s, c, pl.ds(pieces[part][1], pieces[part][2]), :]
                for c in range(2)
                for part in parts
            ],
            axis=0,
        )
        high, low = halves(both)
        cols = jnp.dot(
            jnp.concatenate([high, low], axis=1),
            jnp.concatenate([col_pick[...], col_pick[...]], axis=0),
            preferred_element_type=jnp.float32,
        )
        high, low = halves(cols)
        out = []
        for j in range(slots):
            span = slice(j * window, (j + 1) * window)
            pick = row_pick[span, begin : begin + height]
            field = [
                jnp.concatenate([part[:height, span], part[height:, span]], axis=1)
                for part in (high, low)
            ]
            got = jnp.dot(
                jnp.concatenate([pick, pick], axis=1),
                jnp.concatenate(field, axis=0),
                preferred_element_type=jnp.float32,
            )
            out.append((got[:, :window], got[:, window:]))
        return out

    def both_crops(inside, outside):
        return [(a[0] + b[0], a[1] + b[1]) for a, b in zip(inside, outside)]

    def scatter(it, s, grads, parts):
        begin = pieces[parts[0]][0]
        height = sum(pieces[part][2] for part in parts)
        placed = []
        for j in range(slots):
            put = row_place[begin : begin + height, j * window : (j + 1) * window]
            high, low = halves(jnp.concatenate(grads[j], axis=1))
            got = jnp.dot(
                jnp.concatenate([put, put], axis=1),
                jnp.concatenate([high, low], axis=0),
                preferred_element_type=jnp.float32,
            )
            placed.append(jnp.concatenate([got[:, :window], got[:, window:]], axis=0))
        high, low = halves(jnp.concatenate(placed, axis=1))
        total = jnp.dot(
            jnp.concatenate([high, low], axis=1),
            jnp.concatenate([col_place[...], col_place[...]], axis=0),
            preferred_element_type=jnp.float32,
        )
        for c in range(2):
            for part in parts:
                at, first, length = pieces[part]
                at += c * height - begin
                acc[it, s, c, pl.ds(first, length), :] = total[at : at + length]
        src = acc.at[it, s]
        for part in parts:
            at, first, length = pieces[part]
            rows = pl.ds(first, length)
            re, im = (src[c, rows, 0:LANES] for c in range(2))
            col_out[it, FOLD, s, BACK, pl.ds(at, length), :] = pack_high(re, im)
            re, im = (src[c, rows, lane0 + tile : wide] for c in range(2))
            col_out[it, FOLD, s, AHEAD, pl.ds(at, length), :] = pack_low(re, im)
            for direction in (BACK, AHEAD):
                start(col_copy(it, FOLD, s, part, direction))

    def add_cols(it, s, parts):
        for part in parts:
            at, first, length = pieces[part]
            rows = pl.ds(first, length)
            low = low_lanes((length, LANES))
            got = col_in[it, FOLD, s, AHEAD, pl.ds(at, length), :]
            lanes = slice(lane0, lane0 + LANES)
            acc[it, s, 0, rows, lanes] += jnp.where(low, got, 0.0)
            acc[it, s, 1, rows, lanes] += jnp.where(low, turned(got), 0.0)
            got = col_in[it, FOLD, s, BACK, pl.ds(at, length), :]
            lanes = slice(lane0 + tile - LANES, lane0 + tile)
            acc[it, s, 0, rows, lanes] += jnp.where(low, 0.0, turned(got))
            acc[it, s, 1, rows, lanes] += jnp.where(low, 0.0, got)

    def fold_corners(it, s):
        for direction, part in ((BACK, TOP), (AHEAD, BOTTOM)):
            for side in (BACK, AHEAD):
                col_copy(it, FOLD, s, part, side).wait_recv()
            add_cols(it, s, (part,))
            start(fold_rows(it, s, direction))

    def fold_finish(it, s):
        for direction in (BACK, AHEAD):
            col_copy(it, FOLD, s, MID, direction).wait_recv()
        add_cols(it, s, own)
        for direction in (BACK, AHEAD):
            fold_rows(it, s, direction).wait_recv()
        last = it == ITERS - 1
        for c in range(2):
            for first in range(0, tile, rim):
                total = acc[it, s, c, pl.ds(rim + first, rim), inner]
                if first == 0:
                    total += row_in[it, s, AHEAD, c]
                if first == tile - rim:
                    total += row_in[it, s, BACK, c]
                change = step_size * total
                old = ext[it, s, c, pl.ds(rim + first, rim), inner]
                if last:
                    change_ref[s, c, pl.ds(first, rim), :] = change
                    old_ref[s, c, pl.ds(first, rim), :] = old
                else:
                    ext[it + 1, s, c, pl.ds(rim + first, rim), inner] = old - change

    for s in range(2):
        for direction in (BACK, AHEAD):
            start(halo_rows(0, s, direction))
    for s in range(2):
        for c in range(2):
            ext[0, s, c, rim : rim + tile, inner] = obj_ref[s, c]
        halo_cols(0, s, MID)
    build_picks()

    forward = (right_ref.at[0], left_ref.at[0])
    inverse = (right_ref.at[1], left_ref.at[1])

    prop = phasor(phase_ref[...])
    probe = (probe_ref[0], probe_ref[1])

    for it in range(ITERS):
        halo_arrive(it, 0, own)
        halo_corners(it, 0)
        inside = crop(it, 0, own)
        halo_arrive(it, 0, rims)
        first = both_crops(inside, crop(it, 0, rims))
        waves = [times(probe, a) for a in first]
        waves = [times(prop, f) for f in transform(waves, *forward)]
        halo_corners(it, 1)
        phi = transform(waves, *inverse)
        halo_arrive(it, 1, own)
        inside = crop(it, 1, own)
        halo_arrive(it, 1, rims)
        second = both_crops(inside, crop(it, 1, rims))
        far = transform([times(p, a) for p, a in zip(phi, second)], *forward)
        resid = []
        for j, (re, im) in enumerate(far):
            excess = re * re + im * im - inten_ref[0, 0, j]
            resid.append((excess * re, excess * im))
        back = transform(resid, *inverse)
        grads = [conj_times(p, b) for p, b in zip(phi, back)]
        scatter(it, 1, grads, rims)
        scatter(it, 1, grads, own)
        waves = transform([conj_times(a, b) for a, b in zip(second, back)], *forward)
        fold_corners(it, 1)
        waves = transform([conj_times(prop, f) for f in waves], *inverse)
        grads = [conj_times(probe, g) for g in waves]
        scatter(it, 0, grads, rims)
        scatter(it, 0, grads, own)
        fold_corners(it, 0)
        fold_finish(it, 1)
        if it + 1 < ITERS:
            halo_start(it + 1, 1)
        fold_finish(it, 0)
        if it + 1 < ITERS:
            halo_start(it + 1, 0)
    for copy in sent:
        copy.wait_send()


def local(sizes, window_starts, slot_counts, intensities, probe_field, kernel_phase, object_field):
    tile = object_field.shape[-1]
    window = sizes[2]
    rim = window // 2
    rows_all = tile + 2 * rim
    wide = tile + 2 * LANES
    slots = intensities.shape[2]
    right, left = fourier_tables(window)
    vmem = pl.BlockSpec(memory_space=pltpu.VMEM)
    smem = pl.BlockSpec(memory_space=pltpu.SMEM)
    copies = ITERS * 2 * 2 * 4 * 2
    shape = jax.ShapeDtypeStruct(object_field.shape, jnp.float32)
    old, change = pl.pallas_call(
        functools.partial(kernel, sizes),
        out_shape=(shape, shape),
        in_specs=[smem, smem] + [vmem] * 6,
        out_specs=(vmem, vmem),
        scratch_shapes=[
            pltpu.VMEM((ITERS, 2, 2, rows_all, wide), jnp.float32),
            pltpu.VMEM((ITERS, 2, 2, rows_all, wide), jnp.float32),
            pltpu.VMEM((slots * window, rows_all), jnp.bfloat16),
            pltpu.VMEM((rows_all, slots * window), jnp.bfloat16),
            pltpu.VMEM((wide, slots * window), jnp.bfloat16),
            pltpu.VMEM((slots * window, wide), jnp.bfloat16),
            pltpu.VMEM((ITERS, 2, 2, 2, rows_all, LANES), jnp.float32),
            pltpu.VMEM((ITERS, 2, 2, 2, rows_all, LANES), jnp.float32),
            pltpu.VMEM((ITERS, 2, 2, 2, rim, tile), jnp.float32),
            pltpu.SemaphoreType.DMA((copies,)),
            pltpu.SemaphoreType.DMA((copies,)),
        ],
        compiler_params=pltpu.CompilerParams(
            collective_id=0, has_side_effects=True, vmem_limit_bytes=56 * 1024 * 1024
        ),
    )(
        window_starts,
        slot_counts,
        intensities,
        probe_field,
        kernel_phase,
        jnp.asarray(right),
        jnp.asarray(left),
        object_field,
    )
    return old - change, change / step_size


def solution(mesh):
    in_specs = (
        P("gy", "gx", None, None),
        P("gy", "gx"),
        P("gy", "gx", None, None, None),
        P(),
        P(),
        P(None, None, "gy", "gx"),
    )
    out_specs = (P(None, None, "gy", "gx"), P(None, None, "gy", "gx"))

    def run(*args):
        sizes = (mesh.shape["gy"], mesh.shape["gx"], args[3].shape[-1])
        return jax.shard_map(
            functools.partial(local, sizes),
            mesh=mesh,
            in_specs=in_specs,
            out_specs=out_specs,
            check_vma=False,
        )(*args)

    return run
```

```python
import functools
import math

import jax
import jax.numpy as jnp
import numpy as np
from jax import lax
from jax.experimental import pallas as pl
from jax.experimental.pallas import tpu as pltpu
from jax.sharding import PartitionSpec as P

ITERS = 2
LANES = 128
MESH = pl.DeviceIdType.MESH

step_size = 0.5
HALO, FOLD = 0, 1
BACK, AHEAD = 0, 1
MID, TOP, BOTTOM, ROWS = 0, 1, 2, 3


def split(table):
    high = table.astype(jnp.bfloat16)
    low = (table - high.astype(np.float32)).astype(jnp.bfloat16)
    return high, low


def fourier_tables(window):
    cells = np.arange(window)
    phase = 2.0 * math.pi / window * (cells[:, None] * cells[None, :] % window)
    real = np.cos(phase) / math.sqrt(window)
    rights, lefts = [], []
    for sign in (-1.0, 1.0):
        imag = sign * np.sin(phase) / math.sqrt(window)
        right = np.block([[real, imag], [-imag, real]]).astype(np.float32)
        high, low = split(right)
        rights.append(np.concatenate([high, high, low], axis=0))
        high, low = split(np.ascontiguousarray(right.T))
        lefts.append(np.concatenate([high, low, high], axis=1))
    return np.stack(rights), np.stack(lefts)


def halves(x):
    high = x.astype(jnp.bfloat16)
    low = (x - high.astype(jnp.float32)).astype(jnp.bfloat16)
    return high, low


def transform(fields, right, left):
    size = fields[0][0].shape[0]
    count = len(fields)
    rows = jnp.concatenate([jnp.concatenate(f, axis=1) for f in fields], axis=0)
    high, low = halves(rows)
    rows = jnp.dot(
        jnp.concatenate([high, low, high], axis=1), right[...], preferred_element_type=jnp.float32
    )
    cols = jnp.concatenate(
        [
            jnp.concatenate(
                [
                    rows[n * size : (n + 1) * size, :size],
                    rows[n * size : (n + 1) * size, size:],
                ],
                axis=0,
            )
            for n in range(count)
        ],
        axis=1,
    )
    high, low = halves(cols)
    cols = jnp.dot(
        left[...], jnp.concatenate([high, high, low], axis=0), preferred_element_type=jnp.float32
    )
    return [
        (cols[:size, n * size : (n + 1) * size], cols[size:, n * size : (n + 1) * size])
        for n in range(count)
    ]


def times(a, b):
    return (a[0] * b[0] - a[1] * b[1], a[0] * b[1] + a[1] * b[0])


def conj_times(a, b):
    return (a[0] * b[0] + a[1] * b[1], a[0] * b[1] - a[1] * b[0])


def phasor(angle):
    x = 0.5 * angle
    y = x * x
    sine, cosine = 0.0, 0.0
    for k in range(7, -1, -1):
        sine = sine * y + (-1.0) ** k / math.factorial(2 * k + 1)
        cosine = cosine * y + (-1.0) ** k / math.factorial(2 * k)
    sine = sine * x
    return (1.0 - 2.0 * sine * sine, 2.0 * sine * cosine)


def kernel(
    sizes,
    starts_ref,
    count_ref,
    inten_ref,
    probe_ref,
    phase_ref,
    right_ref,
    left_ref,
    obj_ref,
    old_ref,
    change_ref,
    ext,
    acc,
    row_pick,
    row_place,
    col_pick,
    col_place,
    col_out,
    col_in,
    row_in,
    send_sem,
    recv_sem,
):
    rows_axis, cols_axis, window = sizes
    tile = obj_ref.shape[-1]
    rim = window // 2
    slots = inten_ref.shape[2]
    rows_all = tile + 2 * rim
    lane0 = LANES
    inner = slice(lane0, lane0 + tile)
    wide = tile + 2 * LANES
    my, mx = lax.axis_index("gy"), lax.axis_index("gx")
    up = {"gy": lax.rem(my + rows_axis - 1, rows_axis)}
    down = {"gy": lax.rem(my + 1, rows_axis)}
    west = {"gx": lax.rem(mx + cols_axis - 1, cols_axis)}
    east = {"gx": lax.rem(mx + 1, cols_axis)}

    barrier = pltpu.get_barrier_semaphore()
    for other in (up, down, west, east):
        pl.semaphore_signal(barrier, inc=1, device_id=other, device_id_type=MESH)
    pl.semaphore_wait(barrier, 4)

    def remote(src, dst, it, what, s, part, direction):
        k = ((((it * 2) + what) * 2 + s) * 4 + part) * 2 + direction
        dev = (up, down)[direction] if part == ROWS else (west, east)[direction]
        return pltpu.make_async_remote_copy(
            src_ref=src,
            dst_ref=dst,
            send_sem=send_sem.at[k],
            recv_sem=recv_sem.at[k],
            device_id=dev,
            device_id_type=MESH,
        )

    pieces = {
        MID: (0, rim, tile),
        TOP: (tile, 0, rim),
        BOTTOM: (tile + rim, tile + rim, rim),
    }
    own, rims = (MID,), (TOP, BOTTOM)

    def col_copy(it, what, s, part, direction):
        at = (it, what, s, direction, pl.ds(pieces[part][0], pieces[part][2]))
        return remote(col_out.at[at], col_in.at[at], it, what, s, part, direction)

    def halo_rows(it, s, direction):
        first = 0 if direction == BACK else tile - rim
        if it == 0:
            src = obj_ref.at[s, :, pl.ds(first, rim), :]
        else:
            src = ext.at[it, s, :, pl.ds(rim + first, rim), pl.ds(lane0, tile)]
        land = tile + rim if direction == BACK else 0
        dst = ext.at[it, s, :, pl.ds(land, rim), pl.ds(lane0, tile)]
        return remote(src, dst, it, HALO, s, ROWS, direction)

    def fold_rows(it, s, direction):
        first = 0 if direction == BACK else tile + rim
        src = acc.at[it, s, :, pl.ds(first, rim), pl.ds(lane0, tile)]
        return remote(src, row_in.at[it, s, direction], it, FOLD, s, ROWS, direction)

    def low_lanes(shape):
        return lax.broadcasted_iota(jnp.int32, shape, 1) < rim

    def turned(x):
        return pltpu.roll(x, rim, 1)

    def pack_low(re, im):
        return jnp.where(low_lanes(re.shape), re, turned(im))

    def pack_high(re, im):
        return jnp.where(low_lanes(re.shape), turned(re), im)

    sent = []

    def start(copy):
        copy.start()
        sent.append(copy)

    def halo_cols(it, s, part):
        at, first, length = pieces[part]
        src = ext.at[it, s]
        rows = pl.ds(first, length)
        re, im = (src[c, rows, lane0 : lane0 + LANES] for c in range(2))
        col_out[it, HALO, s, BACK, pl.ds(at, length), :] = pack_low(re, im)
        re, im = (src[c, rows, lane0 + tile - LANES : lane0 + tile] for c in range(2))
        col_out[it, HALO, s, AHEAD, pl.ds(at, length), :] = pack_high(re, im)
        for direction in (BACK, AHEAD):
            start(col_copy(it, HALO, s, part, direction))

    def halo_arrive(it, s, parts):
        for part in parts:
            at, first, length = pieces[part]
            for direction in (BACK, AHEAD):
                col_copy(it, HALO, s, part, direction).wait_recv()
            rows = pl.ds(first, length)
            got = col_in[it, HALO, s, AHEAD, pl.ds(at, length), :]
            ext[it, s, 0, rows, 0:LANES] = turned(got)
            ext[it, s, 1, rows, 0:LANES] = got
            got = col_in[it, HALO, s, BACK, pl.ds(at, length), :]
            ext[it, s, 0, rows, lane0 + tile : wide] = got
            ext[it, s, 1, rows, lane0 + tile : wide] = turned(got)

    def halo_start(it, s):
        for direction in (BACK, AHEAD):
            start(halo_rows(it, s, direction))
        halo_cols(it, s, MID)

    def halo_corners(it, s):
        for direction, part in ((BACK, BOTTOM), (AHEAD, TOP)):
            halo_rows(it, s, direction).wait_recv()
            halo_cols(it, s, part)

    def ones(mask):
        return jnp.where(mask, 1.0, 0.0).astype(jnp.bfloat16)

    def ext_row(k):
        return jnp.where(k < tile, k + rim, jnp.where(k < tile + rim, k - tile, k))

    def build_picks():
        for j in range(slots):
            row = starts_ref[0, 0, 0, j] + rim
            col = starts_ref[0, 0, 1, j] + lane0
            span = slice(j * window, (j + 1) * window)

            def build(shape, large, small, first, order):
                large = order(lax.broadcasted_iota(jnp.int32, shape, large))
                small = lax.broadcasted_iota(jnp.int32, shape, small)
                live = jnp.full(shape, count_ref[0, 0], jnp.int32) > j
                return ones((large - small == first) & live)

            row_pick[span, :] = build((window, rows_all), 1, 0, row, ext_row)
            row_place[:, span] = build((rows_all, window), 0, 1, row, ext_row)
            col_pick[:, span] = build((wide, window), 0, 1, col, lambda k: k)
            col_place[span, :] = build((window, wide), 1, 0, col, lambda k: k)

    def crop(it, s, parts):
        begin = pieces[parts[0]][0]
        height = sum(pieces[part][2] for part in parts)
        both = jnp.concatenate(
            [
                ext[it, s, c, pl.ds(pieces[part][1], pieces[part][2]), :]
                for c in range(2)
                for part in parts
            ],
            axis=0,
        )
        high, low = halves(both)
        cols = jnp.dot(
            jnp.concatenate([high, low], axis=1),
            jnp.concatenate([col_pick[...], col_pick[...]], axis=0),
            preferred_element_type=jnp.float32,
        )
        high, low = halves(cols)
        out = []
        for j in range(slots):
            span = slice(j * window, (j + 1) * window)
            pick = row_pick[span, begin : begin + height]
            field = [
                jnp.concatenate([part[:height, span], part[height:, span]], axis=1)
                for part in (high, low)
            ]
            got = jnp.dot(
                jnp.concatenate([pick, pick], axis=1),
                jnp.concatenate(field, axis=0),
                preferred_element_type=jnp.float32,
            )
            out.append((got[:, :window], got[:, window:]))
        return out

    def both_crops(inside, outside):
        return [(a[0] + b[0], a[1] + b[1]) for a, b in zip(inside, outside)]

    def scatter(it, s, grads, parts):
        begin = pieces[parts[0]][0]
        height = sum(pieces[part][2] for part in parts)
        placed = []
        for j in range(slots):
            put = row_place[begin : begin + height, j * window : (j + 1) * window]
            high, low = halves(jnp.concatenate(grads[j], axis=1))
            got = jnp.dot(
                jnp.concatenate([put, put], axis=1),
                jnp.concatenate([high, low], axis=0),
                preferred_element_type=jnp.float32,
            )
            placed.append(jnp.concatenate([got[:, :window], got[:, window:]], axis=0))
        high, low = halves(jnp.concatenate(placed, axis=1))
        total = jnp.dot(
            jnp.concatenate([high, low], axis=1),
            jnp.concatenate([col_place[...], col_place[...]], axis=0),
            preferred_element_type=jnp.float32,
        )
        for c in range(2):
            for part in parts:
                at, first, length = pieces[part]
                at += c * height - begin
                acc[it, s, c, pl.ds(first, length), :] = total[at : at + length]
        src = acc.at[it, s]
        for part in parts:
            at, first, length = pieces[part]
            rows = pl.ds(first, length)
            re, im = (src[c, rows, 0:LANES] for c in range(2))
            col_out[it, FOLD, s, BACK, pl.ds(at, length), :] = pack_high(re, im)
            re, im = (src[c, rows, lane0 + tile : wide] for c in range(2))
            col_out[it, FOLD, s, AHEAD, pl.ds(at, length), :] = pack_low(re, im)
            for direction in (BACK, AHEAD):
                start(col_copy(it, FOLD, s, part, direction))

    def add_cols(it, s, parts):
        for part in parts:
            at, first, length = pieces[part]
            rows = pl.ds(first, length)
            low = low_lanes((length, LANES))
            got = col_in[it, FOLD, s, AHEAD, pl.ds(at, length), :]
            lanes = slice(lane0, lane0 + LANES)
            acc[it, s, 0, rows, lanes] += jnp.where(low, got, 0.0)
            acc[it, s, 1, rows, lanes] += jnp.where(low, turned(got), 0.0)
            got = col_in[it, FOLD, s, BACK, pl.ds(at, length), :]
            lanes = slice(lane0 + tile - LANES, lane0 + tile)
            acc[it, s, 0, rows, lanes] += jnp.where(low, 0.0, turned(got))
            acc[it, s, 1, rows, lanes] += jnp.where(low, 0.0, got)

    def fold_corners(it, s):
        for direction, part in ((BACK, TOP), (AHEAD, BOTTOM)):
            for side in (BACK, AHEAD):
                col_copy(it, FOLD, s, part, side).wait_recv()
            add_cols(it, s, (part,))
            start(fold_rows(it, s, direction))

    def fold_finish(it, s):
        for direction in (BACK, AHEAD):
            col_copy(it, FOLD, s, MID, direction).wait_recv()
        add_cols(it, s, own)
        for direction in (BACK, AHEAD):
            fold_rows(it, s, direction).wait_recv()
        last = it == ITERS - 1
        for c in range(2):
            for first in range(0, tile, rim):
                total = acc[it, s, c, pl.ds(rim + first, rim), inner]
                if first == 0:
                    total += row_in[it, s, AHEAD, c]
                if first == tile - rim:
                    total += row_in[it, s, BACK, c]
                change = step_size * total
                old = ext[it, s, c, pl.ds(rim + first, rim), inner]
                if last:
                    change_ref[s, c, pl.ds(first, rim), :] = change
                    old_ref[s, c, pl.ds(first, rim), :] = old
                else:
                    ext[it + 1, s, c, pl.ds(rim + first, rim), inner] = old - change

    for s in range(2):
        for direction in (BACK, AHEAD):
            start(halo_rows(0, s, direction))
    for s in range(2):
        for c in range(2):
            ext[0, s, c, rim : rim + tile, inner] = obj_ref[s, c]
        halo_cols(0, s, MID)
    build_picks()

    forward = (right_ref.at[0], left_ref.at[0])
    inverse = (right_ref.at[1], left_ref.at[1])

    prop = phasor(phase_ref[...])
    probe = (probe_ref[0], probe_ref[1])

    for it in range(ITERS):
        halo_arrive(it, 0, own)
        halo_corners(it, 0)
        inside = crop(it, 0, own)
        halo_arrive(it, 0, rims)
        first = both_crops(inside, crop(it, 0, rims))
        waves = [times(probe, a) for a in first]
        waves = [times(prop, f) for f in transform(waves, *forward)]
        halo_corners(it, 1)
        phi = transform(waves, *inverse)
        halo_arrive(it, 1, own)
        inside = crop(it, 1, own)
        halo_arrive(it, 1, rims)
        second = both_crops(inside, crop(it, 1, rims))
        far = transform([times(p, a) for p, a in zip(phi, second)], *forward)
        resid = []
        for j, (re, im) in enumerate(far):
            excess = re * re + im * im - inten_ref[0, 0, j]
            resid.append((excess * re, excess * im))
        back = transform(resid, *inverse)
        grads = [conj_times(p, b) for p, b in zip(phi, back)]
        scatter(it, 1, grads, rims)
        scatter(it, 1, grads, own)
        waves = transform([conj_times(a, b) for a, b in zip(second, back)], *forward)
        fold_corners(it, 1)
        waves = transform([conj_times(prop, f) for f in waves], *inverse)
        grads = [conj_times(probe, g) for g in waves]
        scatter(it, 0, grads, rims)
        scatter(it, 0, grads, own)
        fold_corners(it, 0)
        fold_finish(it, 1)
        fold_finish(it, 0)
        if it + 1 < ITERS:
            halo_start(it + 1, 0)
            halo_start(it + 1, 1)
    for copy in sent:
        copy.wait_send()


def local(sizes, window_starts, slot_counts, intensities, probe_field, kernel_phase, object_field):
    tile = object_field.shape[-1]
    window = sizes[2]
    rim = window // 2
    rows_all = tile + 2 * rim
    wide = tile + 2 * LANES
    slots = intensities.shape[2]
    right, left = fourier_tables(window)
    vmem = pl.BlockSpec(memory_space=pltpu.VMEM)
    smem = pl.BlockSpec(memory_space=pltpu.SMEM)
    copies = ITERS * 2 * 2 * 4 * 2
    shape = jax.ShapeDtypeStruct(object_field.shape, jnp.float32)
    old, change = pl.pallas_call(
        functools.partial(kernel, sizes),
        out_shape=(shape, shape),
        in_specs=[smem, smem] + [vmem] * 6,
        out_specs=(vmem, vmem),
        scratch_shapes=[
            pltpu.VMEM((ITERS, 2, 2, rows_all, wide), jnp.float32),
            pltpu.VMEM((ITERS, 2, 2, rows_all, wide), jnp.float32),
            pltpu.VMEM((slots * window, rows_all), jnp.bfloat16),
            pltpu.VMEM((rows_all, slots * window), jnp.bfloat16),
            pltpu.VMEM((wide, slots * window), jnp.bfloat16),
            pltpu.VMEM((slots * window, wide), jnp.bfloat16),
            pltpu.VMEM((ITERS, 2, 2, 2, rows_all, LANES), jnp.float32),
            pltpu.VMEM((ITERS, 2, 2, 2, rows_all, LANES), jnp.float32),
            pltpu.VMEM((ITERS, 2, 2, 2, rim, tile), jnp.float32),
            pltpu.SemaphoreType.DMA((copies,)),
            pltpu.SemaphoreType.DMA((copies,)),
        ],
        compiler_params=pltpu.CompilerParams(
            collective_id=0, has_side_effects=True, vmem_limit_bytes=56 * 1024 * 1024
        ),
    )(
        window_starts,
        slot_counts,
        intensities,
        probe_field,
        kernel_phase,
        jnp.asarray(right),
        jnp.asarray(left),
        object_field,
    )
    return old - change, change / step_size


def solution(mesh):
    in_specs = (
        P("gy", "gx", None, None),
        P("gy", "gx"),
        P("gy", "gx", None, None, None),
        P(),
        P(),
        P(None, None, "gy", "gx"),
    )
    out_specs = (P(None, None, "gy", "gx"), P(None, None, "gy", "gx"))

    def run(*args):
        sizes = (mesh.shape["gy"], mesh.shape["gx"], args[3].shape[-1])
        return jax.shard_map(
            functools.partial(local, sizes),
            mesh=mesh,
            in_specs=in_specs,
            out_specs=out_specs,
            check_vma=False,
        )(*args)

    return run
```
